32 devices in a mesh: grp: 16 (over z, x, core), shard: 2 (over y).
Axes of the slice: x: 2, y: 2, z: 4, core: 2. Of those that a mesh axis runs over, the one named last changes fastest.
Arguments:
- tokens: bfloat16 [2, 32, 1024, 768], P(None, ('grp', 'shard')), may hold values from -6 to 6
- segments: int32 [2, 32, 1024], P(None, ('grp', 'shard')), may hold values from 0 to 15, never falling along the last dimension, each value on 1 to 512 neighbouring positions
- embed_grad: float32 [2, 32, 1024, 128], P(None, ('grp', 'shard')), may hold values from -67.88225 to 67.88225
- qkv_weight: bfloat16 [768, 2304], P(('grp', 'shard')), may hold values from -0.21875 to 0.21875
- query_bias: bfloat16 [768], P(('grp', 'shard')), may hold values from -3 to 3
- value_bias: bfloat16 [768], P(('grp', 'shard')), may hold values from -3 to 3
- out_weight: bfloat16 [768, 768], P(('grp', 'shard')), may hold values from -0.625 to 0.625
- out_bias: bfloat16 [768], P(('grp', 'shard')), may hold values from -1.75 to 1.75
- norm1_gain: bfloat16 [768], P(('grp', 'shard')), may hold values from 0.25 to 1.75
- norm1_bias: bfloat16 [768], P(('grp', 'shard')), may hold values from -1.75 to 1.75
- up_weight: bfloat16 [768, 3072], P(('grp', 'shard')), may hold values from -0.21875 to 0.21875
- up_bias: bfloat16 [3072], P(('grp', 'shard')), may hold values from -3 to 3
- down_weight: bfloat16 [3072, 768], P(('grp', 'shard')), may hold values from -0.15625 to 0.15625
- down_bias: bfloat16 [768], P(('grp', 'shard')), may hold values from -1.75 to 1.75
- norm2_gain: bfloat16 [768], P(('grp', 'shard')), may hold values from 0.25 to 1.75
- norm2_bias: bfloat16 [768], P(('grp', 'shard')), may hold values from -1.75 to 1.75
- proj_weight: bfloat16 [768, 128], P(('grp', 'shard')), may hold values from -0.21875 to 0.21875
Outputs:
- embed: float32 [2, 32, 1024, 128], P(None, ('grp', 'shard'))
- input_grad: float32 [2, 32, 1024, 768], P(None, ('grp', 'shard'))
- qkv_weight_grad: float32 [768, 2304], P(('grp', 'shard'))
- query_bias_grad: float32 [768], P(('grp', 'shard'))
- value_bias_grad: float32 [768], P(('grp', 'shard'))
- out_weight_grad: float32 [768, 768], P(('grp', 'shard'))
- out_bias_grad: float32 [768], P(('grp', 'shard'))
- norm1_gain_grad: float32 [768], P(('grp', 'shard'))
- norm1_bias_grad: float32 [768], P(('grp', 'shard'))
- up_weight_grad: float32 [768, 3072], P(('grp', 'shard'))
- up_bias_grad: float32 [3072], P(('grp', 'shard'))
- down_weight_grad: float32 [3072, 768], P(('grp', 'shard'))
- down_bias_grad: float32 [768], P(('grp', 'shard'))
- norm2_gain_grad: float32 [768], P(('grp', 'shard'))
- norm2_bias_grad: float32 [768], P(('grp', 'shard'))
- proj_weight_grad: float32 [768, 128], P(('grp', 'shard'))
The draws below stay inside these ranges and needn't reach their ends.
Inputs may be any that keep to these rules, and one draw needn't show every extreme that they name: `segments`: segment numbers never fall along a sequence; every number of 0 to 15 appears, each on 1 to 512 positions, one on exactly 512.
All inputs are finite; a program needn't handle non-finite values.
Results may differ from the reference program's by a relative error of at most 0.017.
Values may be sent and summed in bfloat16 or wider, within the bound.
No kernel may reach another device: no remote copies, remote signals or barrier semaphores. Data moves between devices by JAX's collectives and lax.ppermute only.
A program may use at most 256 MiB of HBM per device.

```python
import math
import jax
import jax.numpy as jnp
import numpy as np
from jax import lax

D = 768
HEADS = 12
HEAD = 64
FF = 3072
EMB = 128
SEQ = 1024
MICRO = 2
SEGS = 16
MOST = 512
NSEQ = 32


def spiked(result, stream_key, source, target, blocks, factor):
    def block_of(position):
        return (jnp.arange(result.shape[position]) // (result.shape[position] // blocks)).reshape((-1,) + (1,) * (result.ndim - 1 - position))

    first = jax.random.permutation(stream_key, blocks)[block_of(target)]
    second = (block_of(target) + blocks // 2) % blocks
    return jnp.where((block_of(source) == first) | (block_of(source) == second), factor * result, result)


def shard_levels(own_key, dims, shards, low, high):
    level, own = 1.0, jax.random.fold_in(own_key, 6)
    for position, blocks in shards:
        steps = jnp.exp(jax.random.uniform(jax.random.fold_in(own, position), (blocks,), jnp.float32, low / len(shards), high / len(shards)))
        level = level * jnp.repeat(steps, dims[position] // blocks).reshape([-1 if axis == position else 1 for axis in range(len(dims))])
    return level


def length_profile(number_of, total, reach, lean):
    portions = [(1 << 20) // math.isqrt(grade ** lean) + 1 for grade in range(2, number_of + 1)]
    spare, counts = total - reach - (number_of - 1), [1] * (number_of - 1)
    while spare > 0:
        movable = [i for i in range(number_of - 1) if counts[i] < reach]
        whole, left = sum([portions[i] for i in movable]), spare
        for i in movable:
            more = min(reach - counts[i], max(1, left * portions[i] // whole), spare)
            counts[i] = counts[i] + more
            spare = spare - more
    return np.array([reach] + counts)


def uneven_parts(stream_key, amount, total, most, slope):
    if amount == 2:
        one = jax.random.randint(stream_key, (), max(1, total - most), min(most, total - 1) + 1)
        return jnp.stack([one, total - one])
    tallies = jnp.asarray(length_profile(amount, total, most, slope), jnp.int32)
    twos = (amount - 1) // 2
    source_of, sink = tallies[1:1 + 2 * twos:2], tallies[2:2 + 2 * twos:2]
    room = jnp.minimum(source_of - 1, most - sink)
    passed = jax.random.randint(jax.random.fold_in(stream_key, 1), (twos,), 0, 1 << 20) % (room + 1)
    tallies = tallies.at[1:1 + 2 * twos:2].set(source_of - passed).at[2:2 + 2 * twos:2].set(sink + passed)
    return tallies[jax.random.permutation(jax.random.fold_in(stream_key, 2), amount)]


def normal_values(key, extent, spread, limit, cuts=(), dtype=jnp.bfloat16):
    loudness = shard_levels(key, extent, cuts, -0.22, 0.18) if cuts else 1.0
    drawn = jax.random.normal(key, extent, jnp.float32) * spread * loudness
    return jnp.minimum(jnp.maximum(drawn, -limit), limit).astype(dtype)


def noise_with(key, dims, deviation, most, cuts, heavy, dtype=jnp.bfloat16):
    result = deviation * jax.random.normal(key, dims, jnp.float32)
    if cuts:
        result = result * shard_levels(key, dims, cuts, -0.22, 0.18)
    return jnp.clip(spiked(result, jax.random.fold_in(key, 3), *heavy), -most, most).astype(dtype)


def setup_inputs(seed: int = 0) -> dict:
    arg_keys = jax.random.split(jax.random.key(seed), 18)
    return {
        "tokens": noise_with(arg_keys[0], (MICRO, NSEQ, SEQ, D), 1.0, 6.0, ((1, 32),), (1, 3, 32, 2.75)),
        "segments": jax.vmap(lambda own: jnp.searchsorted(jnp.cumsum(uneven_parts(own, SEGS, SEQ, MOST, 2)), jnp.arange(SEQ), side="right"))(jax.random.split(arg_keys[1], MICRO * NSEQ)).reshape((MICRO, NSEQ, SEQ)).astype(jnp.int32),
        "embed_grad": normal_values(arg_keys[2], (MICRO, NSEQ, SEQ, EMB), (EMB ** 0.5), 67.88225, ((1, 32),), jnp.float32),
        "qkv_weight": normal_values(arg_keys[3], (D, 3 * D), D ** -0.5, 0.21875, ((0, 32),)),
        "query_bias": normal_values(arg_keys[4], (D,), 0.5, 3.0, ((0, 32),)),
        "value_bias": normal_values(arg_keys[5], (D,), 0.5, 3.0, ((0, 32),)),
        "out_weight": normal_values(arg_keys[6], (D, D), (D // 8) ** -0.5, 0.625, ((0, 32),)),
        "out_bias": normal_values(arg_keys[7], (D,), 0.3, 1.75, ((0, 32),)),
        "norm1_gain": jnp.clip(1.0 + 0.15 * jax.random.normal(arg_keys[8], (D,), jnp.float32), 0.25, 1.75).astype(jnp.bfloat16),
        "norm1_bias": normal_values(arg_keys[9], (D,), 0.3, 1.75, ((0, 32),)),
        "up_weight": normal_values(arg_keys[10], (D, FF), D ** -0.5, 0.21875, ((0, 32),)),
        "up_bias": normal_values(arg_keys[11], (FF,), 0.5, 3.0, ((0, 32),)),
        "down_weight": normal_values(arg_keys[12], (FF, D), (FF // 2) ** -0.5, 0.15625, ((0, 32),)),
        "down_bias": normal_values(arg_keys[13], (D,), 0.3, 1.75, ((0, 32),)),
        "norm2_gain": jnp.clip(1.0 + 0.15 * jax.random.normal(arg_keys[14], (D,), jnp.float32), 0.25, 1.75).astype(jnp.bfloat16),
        "norm2_bias": normal_values(arg_keys[15], (D,), 0.3, 1.75, ((0, 32),)),
        "proj_weight": normal_values(arg_keys[16], (D, EMB), D ** -0.5, 0.21875, ((0, 32),)),
    }


NEG_FILL = -1e+30
NORM_EPS = 1e-12
EMBED_EPS = 1e-06

@jax.custom_vjp
def low(v):
    return lax.optimization_barrier(v.astype(jnp.bfloat16)).astype(jnp.float32)

@jax.custom_vjp
def low_back(v):
    return v

def low_keep(v):
    return (low(v), None)

def low_pass(kept, grad):
    return (grad,)

def back_keep(v):
    return (v, None)

def back_low(kept, grad):
    return (low(grad),)
low.defvjp(low_keep, low_pass)
low_back.defvjp(back_keep, back_low)

def matmul(left, right):
    return jnp.dot(left, right, precision=lax.Precision.HIGHEST, preferred_element_type=jnp.float32)

def layer_norm(hidden, gain, shift):
    center = hidden - lax.optimization_barrier(jnp.mean(hidden, axis=-1, keepdims=True))
    inverse = lax.rsqrt(lax.optimization_barrier(jnp.mean(center * center, axis=-1, keepdims=True)) + NORM_EPS)
    return center * inverse * gain + shift

def split_heads(matrix):
    return matrix.reshape(matrix.shape[0], HEADS, HEAD).transpose(1, 0, 2)

def forward(tokens_in, params, segment_ids):
    qkv_weight, query_bias, value_bias, out_weight, out_bias, norm1_gain, norm1_bias, up_weight, up_bias, down_weight, down_bias, norm2_gain, norm2_bias, proj_weight = params
    width = qkv_weight.shape[0]
    bias_row = jnp.concatenate([query_bias, jnp.zeros_like(query_bias), value_bias])
    joined = matmul(tokens_in, qkv_weight) + bias_row
    queries = low(low_back(joined[:, :width]))
    key_rows = low(low_back(joined[:, width:2 * width]))
    value_rows = low(low_back(joined[:, 2 * width:]))
    same_doc = segment_ids[:, None] == segment_ids[None, :]
    scale = float(HEAD) ** (-0.5)

    def one_head(parts):
        query_head, key_head, value_head = parts
        scores = low_back(matmul(query_head, key_head.T) * scale)
        scores = jnp.where(same_doc, scores, NEG_FILL)
        row_max = lax.optimization_barrier(jnp.max(scores, axis=-1, keepdims=True))
        expo = jnp.exp(scores - row_max)
        attn_probs = low(expo / lax.optimization_barrier(jnp.sum(expo, axis=-1, keepdims=True)))
        return matmul(attn_probs, value_head)
    head_out = lax.map(jax.checkpoint(one_head), (split_heads(queries), split_heads(key_rows), split_heads(value_rows)))
    context = low(low_back(head_out.transpose(1, 0, 2).reshape(tokens_in.shape[0], width)))
    attn_branch = low_back(matmul(context, out_weight) + out_bias)
    first = low(layer_norm(tokens_in + attn_branch, norm1_gain, norm1_bias))
    pre_act = low_back(matmul(first, up_weight) + up_bias)
    act = low(0.5 * pre_act * (1.0 + lax.erf(pre_act * 0.7071067811865476)))
    ffn_branch = low_back(matmul(act, down_weight) + down_bias)
    second = low(layer_norm(first + ffn_branch, norm2_gain, norm2_bias))
    projected = low_back(matmul(second, proj_weight))
    return projected * lax.rsqrt(lax.optimization_barrier(jnp.sum(projected * projected, axis=-1, keepdims=True)) + EMBED_EPS)

def reference(tokens, segments, embed_grad, qkv_weight, query_bias, value_bias, out_weight, out_bias, norm1_gain, norm1_bias, up_weight, up_bias, down_weight, down_bias, norm2_gain, norm2_bias, proj_weight):
    params = tuple((weight.astype(jnp.float32) for weight in (qkv_weight, query_bias, value_bias, out_weight, out_bias, norm1_gain, norm1_bias, up_weight, up_bias, down_weight, down_bias, norm2_gain, norm2_bias, proj_weight)))
    micro_count, seq_count, seq_len, width = tokens.shape
    flat_tokens = tokens.reshape(micro_count * seq_count, seq_len, width).astype(jnp.float32)
    flat_segments = segments.reshape(micro_count * seq_count, seq_len).astype(jnp.int32)
    flat_cotangent = embed_grad.reshape(micro_count * seq_count, seq_len, embed_grad.shape[-1]).astype(jnp.float32)

    def seq_step(running, seq_item):
        seq_tokens, seq_segments, seq_cotangent = seq_item
        embedded, pullback = jax.vjp(lambda token_rows, weights: forward(token_rows, weights, seq_segments), seq_tokens, params)
        token_grad, weight_grads = pullback(seq_cotangent)
        running = tuple((total + part for total, part in zip(running, weight_grads)))
        return (running, (embedded, token_grad))
    start = tuple((jnp.zeros_like(weight) for weight in params))
    totals, (embedded_all, token_grads) = lax.scan(seq_step, start, (flat_tokens, flat_segments, flat_cotangent))
    embed = embedded_all.reshape(embed_grad.shape)
    input_grad = token_grads.reshape(tokens.shape)
    qkv_weight_grad, query_bias_grad, value_bias_grad, out_weight_grad, out_bias_grad, norm1_gain_grad, norm1_bias_grad, up_weight_grad, up_bias_grad, down_weight_grad, down_bias_grad, norm2_gain_grad, norm2_bias_grad, proj_weight_grad = totals
    return (embed, input_grad, qkv_weight_grad, query_bias_grad, value_bias_grad, out_weight_grad, out_bias_grad, norm1_gain_grad, norm1_bias_grad, up_weight_grad, up_bias_grad, down_weight_grad, down_bias_grad, norm2_gain_grad, norm2_bias_grad, proj_weight_grad)
```

```python
import functools

import jax
import jax.numpy as jnp
from jax import lax
from jax.experimental import pallas as pl
from jax.experimental.pallas import tpu as pltpu
from jax.sharding import PartitionSpec as P

F32, BF16 = jnp.float32, jnp.bfloat16
HEADS = 12
HEAD = 64
NEG = -1e30
NORM_EPS = 1e-12
EMBED_EPS = 1e-06
SQRT_HALF = 0.7071067811865476
INV_ROOT_TAU = 0.3989422804014327


def nn(left, right):
    return lax.dot_general(left, right, (((1,), (0,)), ((), ())), preferred_element_type=F32)


def nt(left, right):
    return lax.dot_general(left, right, (((1,), (1,)), ((), ())), preferred_element_type=F32)


def tn(left, right):
    return lax.dot_general(left, right, (((0,), (0,)), ((), ())), preferred_element_type=F32)


def norm_forward(hidden, gain, shift):
    center = hidden - jnp.mean(hidden, axis=-1, keepdims=True)
    inverse = lax.rsqrt(jnp.mean(center * center, axis=-1, keepdims=True) + NORM_EPS)
    normed = center * inverse
    return (normed * gain + shift, normed, inverse)


def norm_backward(grad_out, normed, inverse, gain):
    scaled = grad_out * gain
    return inverse * (
        scaled
        - jnp.mean(scaled, axis=-1, keepdims=True)
        - normed * jnp.mean(scaled * normed, axis=-1, keepdims=True)
    )


def fwd_kernel(lo_ref, hi_ref, segc_ref, segr_ref, q_ref, k_ref, v_ref, ctx_ref, lse_ref, vt, *, qt, kb, pairs):
    s = pl.program_id(0)
    n = q_ref.shape[0]
    low = lax.broadcasted_iota(jnp.int32, (1, 128), 1) < 64
    for p in range(pairs):
        vt[pl.ds(p * 128, 128), :] = v_ref[:, p * 128:(p + 1) * 128].T

    def tile(i, _):
        qs = pl.ds(pl.multiple_of(i * qt, qt), qt)
        segq = segr_ref[0, :, qs]
        lo = lo_ref[s, i]
        cnt = hi_ref[s, i] - lo

        def body(c):
            nk = c * kb
            ks = pl.ds(pl.multiple_of(lo * kb, kb), nk)
            same = segc_ref[0, ks, :] == segq
            for p in range(pairs):
                cols = slice(p * 128, (p + 1) * 128)
                q = q_ref[qs, cols] * jnp.asarray(0.125, BF16)
                zero = jnp.zeros_like(q)
                outs = []
                for hh in range(2):
                    h = 2 * p + hh
                    qm = jnp.where(low, q, zero) if hh == 0 else jnp.where(low, zero, q)
                    sc = jnp.where(same, nt(k_ref[ks, cols], qm), NEG)
                    m = jnp.max(sc, axis=0, keepdims=True)
                    e = jnp.exp(sc - m)
                    l = jnp.sum(e, axis=0, keepdims=True)
                    pv = nn(vt[h * 64:(h + 1) * 64, ks], e.astype(BF16))
                    outs.append(pv / l)
                    lse_ref[0, h:h + 1, qs] = m + jnp.log(l)
                ctx_ref[qs, cols] = jnp.concatenate(outs, axis=0).T.astype(BF16)

        for c in range(1, n // kb + 1):
            pl.when(cnt == c)(functools.partial(body, c))
        return 0

    lax.fori_loop(0, n // qt, tile, 0)


def attn_fwd(joined, segments, lo, hi, *, qt, kb, pairs):
    nseq, n = segments.shape
    width = joined.shape[1] // 3
    nb = width // (128 * pairs)
    segc = segments[:, :, None]
    segr = segments[:, None, :]
    w = 128 * pairs
    return pl.pallas_call(
        functools.partial(fwd_kernel, qt=qt, kb=kb, pairs=pairs),
        grid_spec=pltpu.PrefetchScalarGridSpec(
            num_scalar_prefetch=2, grid=(nseq, nb),
            in_specs=[
                pl.BlockSpec((1, n, 1), lambda s, p, *_: (s, 0, 0)),
                pl.BlockSpec((1, 1, n), lambda s, p, *_: (s, 0, 0)),
                pl.BlockSpec((n, w), lambda s, p, *_: (s, p)),
                pl.BlockSpec((n, w), lambda s, p, *_: (s, nb + p)),
                pl.BlockSpec((n, w), lambda s, p, *_: (s, 2 * nb + p)),
            ],
            out_specs=[
                pl.BlockSpec((n, w), lambda s, p, *_: (s, p)),
                pl.BlockSpec((1, 2 * pairs, n), lambda s, p, *_: (s * nb + p, 0, 0)),
            ],
            scratch_shapes=[pltpu.VMEM((w, n), BF16)],
        ),
        out_shape=[jax.ShapeDtypeStruct((nseq * n, width), BF16),
                   jax.ShapeDtypeStruct((nseq * nb, 2 * pairs, n), F32)],
        compiler_params=pltpu.CompilerParams(vmem_limit_bytes=48 << 20),
        name="attn_fwd",
    )(lo, hi, segc, segr, joined, joined, joined)


def bwd_kernel(lo_ref, hi_ref, segc_ref, segr_ref, q_ref, k_ref, v_ref, ctx_ref, do_ref, lse_ref, out_ref,
               kt, qt_t, dot_t, dk, dv, *, qt, kb, pairs, form):
    s = pl.program_id(0)
    n = q_ref.shape[0]
    low = lax.broadcasted_iota(jnp.int32, (1, 128), 1) < 64
    for p in range(pairs):
        cols = slice(p * 128, (p + 1) * 128)
        kt[pl.ds(p * 128, 128), :] = k_ref[:, cols].T
        if form == "B":
            qt_t[pl.ds(p * 128, 128), :] = (q_ref[:, cols] * jnp.asarray(0.125, BF16)).T
            dot_t[pl.ds(p * 128, 128), :] = do_ref[:, cols].T
    dk[...] = jnp.zeros_like(dk)
    dv[...] = jnp.zeros_like(dv)
    sel = jnp.where((lax.broadcasted_iota(jnp.int32, (8, 128), 1) // 64) == lax.broadcasted_iota(jnp.int32, (8, 128), 0), 1.0, 0.0).astype(F32)

    def tile(i, _):
        qs = pl.ds(pl.multiple_of(i * qt, qt), qt)
        segq = segr_ref[0, :, qs]
        lo = lo_ref[s, i]
        cnt = hi_ref[s, i] - lo

        def body(c):
            nk = c * kb
            ks = pl.ds(pl.multiple_of(lo * kb, kb), nk)
            same = segc_ref[0, ks, :] == segq
            for p in range(pairs):
                cols = slice(p * 128, (p + 1) * 128)
                q = q_ref[qs, cols] * jnp.asarray(0.125, BF16)
                do = do_ref[qs, cols]
                zero = jnp.zeros_like(q)
                prod = do.astype(F32) * ctx_ref[qs, cols].astype(F32)
                d8 = lax.dot_general(sel, prod, (((1,), (1,)), ((), ())), preferred_element_type=F32, precision=lax.Precision.HIGHEST)
                kblk, vblk = k_ref[ks, cols], v_ref[ks, cols]
                dqs = []
                dvs = dks = None
                for hh in range(2):
                    h = 2 * p + hh
                    mask = (lambda t: jnp.where(low, t, zero)) if hh == 0 else (lambda t: jnp.where(low, zero, t))
                    qm, dom = mask(q), mask(do)
                    sc = nt(kblk, qm) - lse_ref[0, h:h + 1, qs]
                    pt = jnp.exp(jnp.where(same, sc, NEG))
                    dp = nt(vblk, dom)
                    ds = (pt * (dp - d8[hh:hh + 1])).astype(BF16)
                    ptl = pt.astype(BF16)
                    hr = slice(h * 64, (h + 1) * 64)
                    if form == "A":
                        a, b = nn(ptl, dom), nn(ds, qm)
                        dvs = a if dvs is None else dvs + a
                        dks = b if dks is None else dks + b
                    else:
                        dv[hr, ks] += nt(dot_t[hr, qs], ptl)
                        dk[hr, ks] += nt(qt_t[hr, qs], ds)
                    dqs.append(nn(kt[hr, ks], ds))
                if form == "A":
                    dv[ks, cols] += dvs
                    dk[ks, cols] += dks
                out_ref[0, qs, cols] = (jnp.concatenate(dqs, axis=0).T * 0.125).astype(BF16)

        for c in range(1, n // kb + 1):
            pl.when(cnt == c)(functools.partial(body, c))
        return 0

    lax.fori_loop(0, n // qt, tile, 0)
    if form == "A":
        out_ref[1] = dk[...].astype(BF16)
        out_ref[2] = dv[...].astype(BF16)
    else:
        for p in range(pairs):
            cols = slice(p * 128, (p + 1) * 128)
            out_ref[1, :, cols] = dk[cols, :].T.astype(BF16)
            out_ref[2, :, cols] = dv[cols, :].T.astype(BF16)


def attn_bwd(joined, ctx, dctx, lse, segments, lo, hi, *, qt, kb, pairs, form="A"):
    nseq, n = segments.shape
    width = joined.shape[1] // 3
    nb = width // (128 * pairs)
    segc = segments[:, :, None]
    segr = segments[:, None, :]
    w = 128 * pairs
    acc = (n, w) if form == "A" else (w, n)
    tr = (w, n) if form == "B" else (8, 128)
    return pl.pallas_call(
        functools.partial(bwd_kernel, qt=qt, kb=kb, pairs=pairs, form=form),
        grid_spec=pltpu.PrefetchScalarGridSpec(
            num_scalar_prefetch=2, grid=(nseq, nb),
            in_specs=[
                pl.BlockSpec((1, n, 1), lambda s, p, *_: (s, 0, 0)),
                pl.BlockSpec((1, 1, n), lambda s, p, *_: (s, 0, 0)),
                pl.BlockSpec((n, w), lambda s, p, *_: (s, p)),
                pl.BlockSpec((n, w), lambda s, p, *_: (s, nb + p)),
                pl.BlockSpec((n, w), lambda s, p, *_: (s, 2 * nb + p)),
                pl.BlockSpec((n, w), lambda s, p, *_: (s, p)),
                pl.BlockSpec((n, w), lambda s, p, *_: (s, p)),
                pl.BlockSpec((1, 2 * pairs, n), lambda s, p, *_: (s * nb + p, 0, 0)),
            ],
            out_specs=pl.BlockSpec((3, n, w), lambda s, p, *_: (0, s, p)),
            scratch_shapes=[pltpu.VMEM((w, n), BF16), pltpu.VMEM(tr, BF16), pltpu.VMEM(tr, BF16), pltpu.VMEM(acc, F32), pltpu.VMEM(acc, F32)],
        ),
        out_shape=jax.ShapeDtypeStruct((3, nseq * n, width), BF16),
        compiler_params=pltpu.CompilerParams(vmem_limit_bytes=56 << 20),
        name="attn_bwd",
    )(lo, hi, segc, segr, joined, joined, joined, ctx, dctx, lse)


def ranges(segments, qt, kb):
    first = segments[:, ::qt]
    last = segments[:, qt - 1::qt]
    lo = jnp.sum(segments[:, None, :] < first[:, :, None], axis=-1, dtype=jnp.int32) // kb
    hi = (jnp.sum(segments[:, None, :] <= last[:, :, None], axis=-1, dtype=jnp.int32) + kb - 1) // kb
    return lo, hi


def layer_pass(full, tokens_in, segments, cotangent):
    (qkv_weight, query_bias, value_bias, out_weight, out_bias, norm1_gain, norm1_bias, up_weight, up_bias,
     down_weight, down_bias, norm2_gain, norm2_bias, proj_weight) = full
    width = qkv_weight.shape[0]
    gain_one = norm1_gain.astype(F32)
    gain_two = norm2_gain.astype(F32)
    bias_row = jnp.concatenate([query_bias, jnp.zeros_like(query_bias), value_bias]).astype(F32)
    joined = (nn(tokens_in, qkv_weight) + bias_row).astype(BF16)
    lo_f, hi_f = ranges(segments, 512, 256)
    context, lse = attn_fwd(joined, segments, lo_f, hi_f, qt=512, kb=256, pairs=2)
    attn_branch = nn(context, out_weight) + out_bias.astype(F32)
    first_out, first_normed, first_inverse = norm_forward(
        tokens_in.astype(F32) + attn_branch, gain_one, norm1_bias.astype(F32)
    )
    first_low = first_out.astype(BF16)
    pre_act = nn(first_low, up_weight) + up_bias.astype(F32)
    normal_cdf = 0.5 * (1.0 + lax.erf(pre_act * SQRT_HALF))
    act_low = (pre_act * normal_cdf).astype(BF16)
    act_slope = (normal_cdf + pre_act * jnp.exp(-0.5 * pre_act * pre_act) * INV_ROOT_TAU).astype(BF16)
    ffn_branch = nn(act_low, down_weight) + down_bias.astype(F32)
    second_out, second_normed, second_inverse = norm_forward(
        first_low.astype(F32) + ffn_branch, gain_two, norm2_bias.astype(F32)
    )
    second_low = second_out.astype(BF16)
    projected = nn(second_low, proj_weight)
    inv_length = lax.rsqrt(jnp.sum(projected * projected, axis=-1, keepdims=True) + EMBED_EPS)
    embedded = projected * inv_length
    grad_proj = (
        inv_length * cotangent
        - projected * inv_length**3 * jnp.sum(cotangent * projected, axis=-1, keepdims=True)
    ).astype(BF16)
    proj_grad = tn(second_low, grad_proj)
    grad_second = nt(grad_proj, proj_weight)
    gain_two_grad = jnp.sum(grad_second * second_normed, axis=0)
    shift_two_grad = jnp.sum(grad_second, axis=0)
    grad_res_two = norm_backward(grad_second, second_normed, second_inverse, gain_two)
    grad_ffn = grad_res_two.astype(BF16)
    down_bias_grad = jnp.sum(grad_ffn.astype(F32), axis=0)
    down_grad = tn(act_low, grad_ffn)
    grad_pre = (nt(grad_ffn, down_weight) * act_slope.astype(F32)).astype(BF16)
    up_bias_grad = jnp.sum(grad_pre.astype(F32), axis=0)
    up_grad = tn(first_low, grad_pre)
    grad_first = grad_res_two + nt(grad_pre, up_weight)
    gain_one_grad = jnp.sum(grad_first * first_normed, axis=0)
    shift_one_grad = jnp.sum(grad_first, axis=0)
    grad_res_one = norm_backward(grad_first, first_normed, first_inverse, gain_one)
    grad_attn = grad_res_one.astype(BF16)
    out_bias_grad = jnp.sum(grad_attn.astype(F32), axis=0)
    out_grad = tn(context, grad_attn)
    grad_context = nt(grad_attn, out_weight).astype(BF16)
    lo_b, hi_b = ranges(segments, 256, 256)
    grad_joined = attn_bwd(joined, context, grad_context, lse, segments, lo_b, hi_b, qt=256, kb=256, pairs=2, form="B")
    query_bias_grad = jnp.sum(grad_joined[0].astype(F32), axis=0)
    value_bias_grad = jnp.sum(grad_joined[2].astype(F32), axis=0)
    qkv_grad = jnp.concatenate([tn(tokens_in, grad_joined[i]) for i in range(3)], axis=1)
    input_grad = grad_res_one
    for i in range(3):
        input_grad = input_grad + nt(grad_joined[i], qkv_weight[:, i * width:(i + 1) * width])
    grads = (qkv_grad, query_bias_grad, value_bias_grad, out_grad, out_bias_grad, gain_one_grad, shift_one_grad,
             up_grad, up_bias_grad, down_grad, down_bias_grad, gain_two_grad, shift_two_grad, proj_grad)
    return embedded, input_grad, grads


AXES = ("grp", "shard")


def local(tokens, segments, embed_grad, *pieces):
    micro, nseq, length, width = tokens.shape
    full = tuple(lax.all_gather(piece, AXES, axis=0, tiled=True) for piece in pieces)
    embedded, input_grad, grads = layer_pass(
        full,
        tokens.reshape(micro * nseq * length, width),
        segments.reshape(micro * nseq, length),
        embed_grad.reshape(micro * nseq * length, embed_grad.shape[-1]),
    )
    reduced = lax.psum_scatter(grads, AXES, scatter_dimension=0, tiled=True)
    return (embedded.reshape(embed_grad.shape), input_grad.reshape(tokens.shape)) + tuple(reduced)


def solution(mesh):
    placed = (
        P(None, ("grp", "shard"), None, None),
        P(None, ("grp", "shard"), None),
        P(None, ("grp", "shard"), None, None),
        P(("grp", "shard"), None),
        P(("grp", "shard")),
        P(("grp", "shard")),
        P(("grp", "shard"), None),
        P(("grp", "shard")),
        P(("grp", "shard")),
        P(("grp", "shard")),
        P(("grp", "shard"), None),
        P(("grp", "shard")),
        P(("grp", "shard"), None),
        P(("grp", "shard")),
        P(("grp", "shard")),
        P(("grp", "shard")),
        P(("grp", "shard"), None),
    )
    return jax.shard_map(
        local,
        mesh=mesh,
        in_specs=placed,
        out_specs=(
            P(None, ("grp", "shard"), None, None),
            P(None, ("grp", "shard"), None, None),
            P(("grp", "shard"), None),
            P(("grp", "shard")),
            P(("grp", "shard")),
            P(("grp", "shard"), None),
            P(("grp", "shard")),
            P(("grp", "shard")),
            P(("grp", "shard")),
            P(("grp", "shard"), None),
            P(("grp", "shard")),
            P(("grp", "shard"), None),
            P(("grp", "shard")),
            P(("grp", "shard")),
            P(("grp", "shard")),
            P(("grp", "shard"), None),
        ),
        check_vma=False,
    )
```
